32 devices in a mesh: seq: 16 (over z, x, core), head: 2 (over y).
Axes of the slice: x: 2, y: 2, z: 4, core: 2. Of those that a mesh axis runs over, the one named last changes fastest.
Arguments:
- queries: bfloat16 [6144, 2048], P('seq', 'head'), may hold values from -6 to 6
- keys: bfloat16 [6144, 256], P('seq', 'head'), may hold values from -6 to 6
- values: bfloat16 [6144, 256], P('seq', 'head'), may hold values from -6 to 6
- windows: int32 [2], P('head'), may hold values from 256 to 4096, as said below
- out_weight: bfloat16 [2048, 8192], P('head', 'seq'), may hold values from -0.125 to 0.125
Outputs:
- projected: bfloat16 [6144, 8192], P('seq', 'head')
The draws below stay inside these ranges and needn't reach their ends.
Inputs may be any that keep to these rules, and one draw needn't show every extreme that they name: `windows`: every window is a multiple of 128; in every draw some group has exactly 4096, and where there are three groups or more another has exactly 256.
All inputs are finite; a program needn't handle non-finite values.
Results may differ from the reference program's by a relative error of at most 0.014.
Values may be sent and summed in bfloat16 or wider, within the bound.
No kernel may reach another device: no remote copies, remote signals or barrier semaphores. Data moves between devices by JAX's collectives and lax.ppermute only.
A program may use at most 128 MiB of HBM per device.

```python
import math
import jax
import jax.numpy as jnp
from jax import lax

D = 8192
DH = 128
QPG = 8
TOK_DEV = 384
WMAX = 4096
WMIN = 256
WSTEP = 128
KVH = 2
HEADS = 16
TOKENS = 6144


def draw_queries(key, part):
    first_key_index = jax.random.fold_in(key, 1)
    shape = (TOKENS, KVH, QPG, DH)
    base = jax.random.truncated_normal(first_key_index, -4.0, 4.0, shape, jnp.float32)
    return base.reshape(TOKENS, KVH * QPG * DH).astype(jnp.bfloat16)


def draw_keys(key, part):
    first_key_index = jax.random.fold_in(key, 2)
    shape = (TOKENS, KVH, DH)
    base = jax.random.truncated_normal(first_key_index, -4.0, 4.0, shape, jnp.float32)
    return base.reshape(TOKENS, KVH * DH).astype(jnp.bfloat16)


def draw_windows(key, part):
    counts = jax.random.randint(jax.random.fold_in(key, 5), (KVH,), WMIN // WSTEP, WMAX // WSTEP + 1, jnp.int32)
    spans = counts * WSTEP
    order = jax.random.permutation(jax.random.fold_in(key, 6), KVH)
    spans = spans.at[order[0]].set(WMAX)
    if KVH > 2:
        spans = spans.at[order[1]].set(WMIN)
    return spans.astype(jnp.int32)


def block_levels(own_key, shape, cuts, least, top_value):
    loudness, own = 1.0, jax.random.fold_in(own_key, 6)
    for dim, shards_of in cuts:
        heights = jnp.exp(jax.random.uniform(jax.random.fold_in(own, dim), (shards_of,), jnp.float32, least / len(cuts), top_value / len(cuts)))
        loudness = loudness * jnp.repeat(heights, shape[dim] // shards_of).reshape([-1 if axis == dim else 1 for axis in range(len(shape))])
    return loudness


def noise(key, shape, scale, most, split=(), held_as=jnp.bfloat16):
    result = jax.random.normal(key, shape, jnp.float32) * scale
    if len(split) > 0:
        result = block_levels(key, shape, split, -0.22, 0.18) * result
    return jnp.clip(result, min=-most, max=most).astype(held_as)


def setup_inputs(seed: int = 0) -> dict:
    splits = jax.random.split(jax.random.key(seed), 6)
    return {
        "queries": draw_queries(jax.random.fold_in(splits[5], 71), 0),
        "keys": draw_keys(jax.random.fold_in(splits[5], 71), 0),
        "values": noise(splits[2], (TOKENS, KVH * DH), 1.0, 6.0, ((0, 16), (1, 2))),
        "windows": draw_windows(jax.random.fold_in(splits[5], 71), 0),
        "out_weight": noise(splits[4], (HEADS * DH, D), (HEADS * DH) ** -0.5, 0.125, ((0, 2), (1, 16))),
    }


def reference(queries, keys, values, windows, out_weight):
    blocks_total = TOKENS // TOK_DEV
    halo_len = (WMAX + TOK_DEV - 2) // TOK_DEV * TOK_DEV
    score_scale = 1.0 / math.sqrt(DH)
    key_pad = jnp.concatenate([jnp.zeros((halo_len, KVH * DH), keys.dtype), keys], 0)
    value_pad = jnp.concatenate([jnp.zeros((halo_len, KVH * DH), values.dtype), values], 0)
    spans = windows.astype(jnp.int32)

    def single_block_attend(block_index):
        first = (block_index * TOK_DEV).astype(jnp.int32)
        query_block = lax.dynamic_slice_in_dim(queries, first, TOK_DEV, 0).reshape(TOK_DEV, KVH, QPG, DH).astype(jnp.float32)
        key_block = lax.dynamic_slice_in_dim(key_pad, first, halo_len + TOK_DEV, 0).reshape(halo_len + TOK_DEV, KVH, DH).astype(jnp.float32)
        value_block = lax.dynamic_slice_in_dim(value_pad, first, halo_len + TOK_DEV, 0).reshape(halo_len + TOK_DEV, KVH, DH).astype(jnp.float32)
        scores = jnp.einsum('igpd,jgd->gpij', query_block, key_block) * score_scale
        query_pos = first + jnp.arange(TOK_DEV, dtype=jnp.int32)
        key_pos = first - halo_len + jnp.arange(halo_len + TOK_DEV, dtype=jnp.int32)
        allowed = (key_pos[None, None, :] <= query_pos[None, :, None]) & (key_pos[None, None, :] > query_pos[None, :, None] - spans[:, None, None]) & (key_pos[None, None, :] >= 0)
        allowed = allowed[:, None]
        masked = jnp.where(allowed, scores, -1e+30)
        peak_score_running = lax.optimization_barrier(jnp.max(masked, axis=-1, keepdims=True))
        weights = jnp.where(allowed, jnp.exp(scores - peak_score_running), 0.0)
        total = lax.optimization_barrier(jnp.sum(weights, axis=-1))
        rounded = lax.optimization_barrier(weights.astype(jnp.bfloat16)).astype(jnp.float32)
        mixed = jnp.einsum('gpij,jgd->igpd', rounded, value_block)
        mixed = mixed / jnp.transpose(total, (2, 0, 1))[..., None]
        return mixed.astype(jnp.bfloat16).reshape(TOK_DEV, KVH * QPG * DH)
    attended = lax.map(single_block_attend, jnp.arange(blocks_total, dtype=jnp.int32))
    attended = attended.reshape(TOKENS, KVH * QPG * DH)
    return jnp.dot(attended, out_weight, preferred_element_type=jnp.float32).astype(jnp.bfloat16)
```

```python
import math

import jax
import jax.numpy as jnp
from jax import lax
from jax.experimental import pallas as pl
from jax.experimental.pallas import tpu as pltpu
from jax.sharding import PartitionSpec as P

DH = 128
WMAX = 4096
TQ = 128
CH = 512
MIB = 1024 * 1024


SMEM = pl.BlockSpec(memory_space=pltpu.SMEM)
VMEM = pl.BlockSpec(memory_space=pltpu.VMEM)
ANY = pl.BlockSpec(memory_space=pl.ANY)


def aligned(i):
    return pl.multiple_of(i, 128)


def lay_out_keys(packs, offsets, span):
    rows = packs[0].shape[0] // offsets[0].shape[0]
    where = [(i, k) for i, o in enumerate(offsets) for k in range(o.shape[0])]
    blocks = len(where)
    total = blocks * rows
    pad = CH + rows

    def kernel(start_ref, span_ref, *refs):
        pack_refs = refs[: len(packs)]
        kt_ref, va_ref, held, sem = refs[len(packs) :]
        copies = [
            pltpu.make_async_copy(
                pack_refs[i].at[pl.ds(k * rows, rows)],
                held.at[pl.ds(aligned(start_ref[n]), rows)],
                sem.at[n],
            )
            for n, (i, k) in enumerate(where)
        ]
        for copy in copies:
            copy.start()
        kt_ref[:, :pad] = jnp.zeros((2 * DH, pad), jnp.bfloat16)
        va_ref[:pad, :] = jnp.zeros((pad, 2 * DH), jnp.bfloat16)
        first = lax.broadcasted_iota(jnp.int32, (rows, DH), 1) == 0
        ones = jnp.where(first, 1.0, 0.0).astype(jnp.bfloat16)
        for copy in copies:
            copy.wait()

        def one(b, _):
            r = aligned(b * rows)
            to = pl.ds(aligned(pad + r), rows)

            @pl.when((r < span_ref[1]) & (r + rows + CH > span_ref[0]))
            def _():
                kt = held[pl.ds(r, rows), :DH].T
                kt_ref[:DH, to] = kt
                kt_ref[DH:, to] = kt
                va_ref[to, :DH] = held[pl.ds(r, rows), DH:]
                va_ref[to, DH:] = ones

            return 0

        lax.fori_loop(0, blocks, one, 0)

    return pl.pallas_call(
        kernel,
        out_shape=(
            jax.ShapeDtypeStruct((2 * DH, pad + total), jnp.bfloat16),
            jax.ShapeDtypeStruct((pad + total, 2 * DH), jnp.bfloat16),
        ),
        in_specs=[SMEM, SMEM] + [ANY] * len(packs),
        out_specs=(VMEM, VMEM),
        scratch_shapes=[
            pltpu.VMEM((total, 2 * DH), jnp.bfloat16),
            pltpu.SemaphoreType.DMA((blocks,)),
        ],
        compiler_params=pltpu.CompilerParams(vmem_limit_bytes=24 * MIB),
        name="lay_out_keys",
    )(jnp.concatenate(offsets), span, *packs)


def attend(queries, kt, va, span, tiles, earlier=None):
    heads = queries.shape[1] // DH
    tok_rows = queries.shape[0]
    rows = heads * TQ
    chunks = -(-(WMAX + TQ) // CH)
    scale = math.log2(math.e) / math.sqrt(DH)
    pad = CH + tok_rows

    def kernel(span_ref, q_ref, kt_hbm, va_hbm, *refs):
        refs = refs[0 if earlier is None else 1 :]
        o_ref, kt_v, va_v, q0, q1, s0, s1, m0, m1, acc, o_v, sem = refs
        qa, scores, tops = (q0, q1), (s0, s1), (m0, m1)
        kt_copy = pltpu.make_async_copy(kt_hbm, kt_v, sem.at[0])
        va_copy = pltpu.make_async_copy(va_hbm, va_v, sem.at[1])
        kt_copy.start()
        va_copy.start()
        start, win = span_ref[2], span_ref[3]

        def chunk_count(i):
            reach = jnp.minimum(win + TQ, start + (tiles[i] + 1) * TQ)
            return (reach + CH - 1) // CH

        def load_q(i):
            t = tiles[i]
            for p in range(heads):
                x = q_ref[t * TQ : (t + 1) * TQ, p * DH : (p + 1) * DH].astype(jnp.float32) * scale
                high = x.astype(jnp.bfloat16)
                qa[i % 2][p * TQ : (p + 1) * TQ, :DH] = high
                qa[i % 2][p * TQ : (p + 1) * TQ, DH:] = (x - high.astype(jnp.float32)).astype(
                    jnp.bfloat16
                )

        def key_start(i, j):
            return start + (tiles[i] + 1) * TQ - (j + 1) * CH

        def score(i, j, masked):
            ks = key_start(i, j)
            s = jnp.dot(
                qa[i % 2][...],
                kt_v[:, pl.ds(aligned(ks + pad), CH)],
                preferred_element_type=jnp.float32,
            )
            if masked:
                kp = ks + lax.broadcasted_iota(jnp.int32, (TQ, CH), 1)
                qp = start + tiles[i] * TQ + lax.broadcasted_iota(jnp.int32, (TQ, CH), 0)
                bias = jnp.where((kp <= qp) & (kp > qp - win) & (kp >= 0), 0.0, -1e30)
                s = (s.reshape(heads, TQ, CH) + bias[None]).reshape(rows, CH)
            scores[i % 2][j] = s
            top = tops[i % 2][...]
            for a in range(CH // 128):
                top = jnp.maximum(top, s[:, a * 128 : (a + 1) * 128])
            tops[i % 2][...] = top

        def weigh(i, j, top):
            p = jnp.exp2(scores[i % 2][j] - top).astype(jnp.bfloat16)
            acc[...] += jnp.dot(
                p,
                va_v[pl.ds(aligned(key_start(i, j) + pad), CH), :],
                preferred_element_type=jnp.float32,
            )

        kt_copy.wait()
        for i in range(len(tiles) + 1):
            if i > 0:
                top = jnp.max(tops[(i - 1) % 2][...], axis=1, keepdims=True)
                top = jnp.broadcast_to(top, (rows, CH))
                acc[...] = jnp.zeros_like(acc)
            if i < len(tiles):
                load_q(i)
                tops[i % 2][...] = jnp.full((rows, 128), -1e30, jnp.float32)

            def each(low, high, *steps):
                def inner(j, _):
                    for step in steps:
                        step(j)
                    return 0

                lax.fori_loop(low, high, inner, 0)

            scoring = lambda j, i=i: score(i, j, False)
            weighing = lambda j, i=i, top=(top if i > 0 else None): weigh(i - 1, j, top)
            if i < len(tiles):
                n = chunk_count(i)
                score(i, 0, True)
            if i > 0:
                before = chunk_count(i - 1)
                weighing(0)
            if i == 0:
                each(1, n - 1, scoring)
            elif i == len(tiles):
                each(1, before, weighing)
            else:
                shared = jnp.minimum(n - 1, before)
                each(1, shared, scoring, weighing)
                each(jnp.maximum(shared, 1), n - 1, scoring)
                each(jnp.maximum(shared, 1), before, weighing)
            if i < len(tiles):

                @pl.when(n > 1)
                def _():
                    score(i, n - 1, True)

            if i == 0:
                va_copy.wait()
            else:
                t = tiles[i - 1]
                o = acc[:, :DH] / acc[:, DH : DH + 1]
                for p in range(heads):
                    o_v[(i - 1) * TQ : i * TQ, p * DH : (p + 1) * DH] = o[
                        p * TQ : (p + 1) * TQ
                    ].astype(o_v.dtype)
        done = pltpu.make_async_copy(
            o_v, o_ref.at[pl.ds(tiles[0] * TQ, len(tiles) * TQ)], sem.at[0]
        )
        done.start()
        done.wait()

    f32 = jnp.float32
    more = [] if earlier is None else [earlier]
    return pl.pallas_call(
        kernel,
        out_shape=jax.ShapeDtypeStruct(queries.shape, jnp.bfloat16),
        in_specs=[SMEM, VMEM, ANY, ANY] + [ANY] * len(more),
        out_specs=ANY,
        scratch_shapes=[
            pltpu.VMEM(kt.shape, jnp.bfloat16),
            pltpu.VMEM(va.shape, jnp.bfloat16),
            pltpu.VMEM((rows, 2 * DH), jnp.bfloat16),
            pltpu.VMEM((rows, 2 * DH), jnp.bfloat16),
            pltpu.VMEM((chunks, rows, CH), f32),
            pltpu.VMEM((chunks, rows, CH), f32),
            pltpu.VMEM((rows, 128), f32),
            pltpu.VMEM((rows, 128), f32),
            pltpu.VMEM((rows, 2 * DH), f32),
            pltpu.VMEM((len(tiles) * TQ, heads * DH), jnp.bfloat16),
            pltpu.SemaphoreType.DMA((2,)),
        ],
        input_output_aliases={4: 0} if more else {},
        compiler_params=pltpu.CompilerParams(vmem_limit_bytes=56 * MIB),
        name="attend",
    )(span, queries, kt, va, *more)


def project(attended, units, columns, width, earlier=None):
    tok_rows, depth = attended[0].shape
    cols = units[0][0][0].shape[1]
    flat = [piece for unit in units for side in unit for piece in side]

    def kernel(col_ref, *refs):
        a_refs = refs[:4]
        w_refs = refs[4 : 4 + len(flat)]
        refs = refs[4 + len(flat) + (0 if earlier is None else 1) :]
        out_ref, send_ref, a_v, w_v, o_v, a_sem, w_sem, o_sem = refs
        a_copies = [
            pltpu.make_async_copy(
                a_refs[2 * side + k],
                a_v.at[pl.ds(side * tok_rows, tok_rows), pl.ds(k * depth, depth)],
                a_sem.at[2 * side + k],
            )
            for side in (0, 1)
            for k in (0, 1)
        ]
        w_copies = []
        n = 0
        for u, unit in enumerate(units):
            row, mine = 0, []
            for side in unit:
                for piece in side:
                    mine.append(
                        pltpu.make_async_copy(
                            w_refs[n], w_v.at[u, pl.ds(row, piece.shape[0])], w_sem.at[n]
                        )
                    )
                    row += piece.shape[0]
                    n += 1
            w_copies.append(mine)
        for copy in w_copies[0] + a_copies:
            copy.start()
        for mine in w_copies[1:]:
            for copy in mine:
                copy.start()
        for copy in a_copies:
            copy.wait()
        out_copies = []
        for u in range(len(units)):
            for copy in w_copies[u]:
                copy.wait()
            o_v[u] = jnp.dot(a_v[...], w_v[u], preferred_element_type=jnp.float32).astype(
                jnp.bfloat16
            )
            mine = pltpu.make_async_copy(
                o_v.at[u, pl.ds(0, tok_rows)],
                out_ref.at[:, pl.ds(aligned(col_ref[u] * cols), cols)],
                o_sem.at[2 * u],
            )
            theirs = pltpu.make_async_copy(
                o_v.at[u, pl.ds(tok_rows, tok_rows)],
                send_ref.at[u],
                o_sem.at[2 * u + 1],
            )
            mine.start()
            theirs.start()
            out_copies += [mine, theirs]
        for copy in out_copies:
            copy.wait()

    more = [] if earlier is None else [earlier]
    return pl.pallas_call(
        kernel,
        out_shape=(
            jax.ShapeDtypeStruct((tok_rows, width), jnp.bfloat16),
            jax.ShapeDtypeStruct((len(units), tok_rows, cols), jnp.bfloat16),
        ),
        in_specs=[SMEM] + [ANY] * (4 + len(flat) + len(more)),
        out_specs=(ANY, ANY),
        scratch_shapes=[
            pltpu.VMEM((2 * tok_rows, 2 * depth), jnp.bfloat16),
            pltpu.VMEM((len(units), 2 * depth, cols), jnp.bfloat16),
            pltpu.VMEM((len(units), 2 * tok_rows, cols), jnp.bfloat16),
            pltpu.SemaphoreType.DMA((4,)),
            pltpu.SemaphoreType.DMA((len(flat),)),
            pltpu.SemaphoreType.DMA((2 * len(units),)),
        ],
        input_output_aliases={5 + len(flat): 0} if more else {},
        compiler_params=pltpu.CompilerParams(vmem_limit_bytes=32 * MIB),
        name="project",
    )(columns, *attended, *flat, *more)


def put_blocks(out, received, columns):
    cols = received[0].shape[2]
    where = [(i, k) for i, r in enumerate(received) for k in range(r.shape[0])]

    def kernel(col_ref, *refs):
        r_refs = refs[: len(received)]
        out_ref, held, in_sem, out_sem = refs[len(received) + 1 :]
        ins = [
            pltpu.make_async_copy(r_refs[i].at[k], held.at[n], in_sem.at[n])
            for n, (i, k) in enumerate(where)
        ]
        outs = [
            pltpu.make_async_copy(
                held.at[n],
                out_ref.at[:, pl.ds(aligned(col_ref[n] * cols), cols)],
                out_sem.at[n],
            )
            for n in range(len(where))
        ]
        for copy in ins:
            copy.start()
        for came, copy in zip(ins, outs):
            came.wait()
            copy.start()
        for copy in outs:
            copy.wait()

    return pl.pallas_call(
        kernel,
        out_shape=jax.ShapeDtypeStruct(out.shape, out.dtype),
        in_specs=[SMEM] + [ANY] * (len(received) + 1),
        out_specs=ANY,
        scratch_shapes=[
            pltpu.VMEM((len(where), out.shape[0], cols), out.dtype),
            pltpu.SemaphoreType.DMA((len(where),)),
            pltpu.SemaphoreType.DMA((len(where),)),
        ],
        input_output_aliases={1 + len(received): 0},
        compiler_params=pltpu.CompilerParams(vmem_limit_bytes=16 * MIB),
        name="put_blocks",
    )(columns, *received, out)


def swap(block, distance):
    n = lax.axis_size("seq")
    return lax.ppermute(block, "seq", [(i, i ^ distance) for i in range(n)])


def swap_head(block):
    return lax.ppermute(block, "head", [(0, 1), (1, 0)])


def body_any(queries, keys, values, windows, out_weight):
    tok_rows = queries.shape[0]
    n = lax.axis_size("seq")
    groups = keys.shape[1] // DH
    per_group = queries.shape[1] // groups
    start = lax.axis_index("seq") * tok_rows
    attended = []
    for g in range(groups):
        lanes = slice(g * DH, (g + 1) * DH)
        pair = jnp.concatenate([keys[:, lanes], values[:, lanes]], axis=1)
        pack = lax.all_gather(pair, "seq", axis=0, tiled=True)
        span = jnp.stack([start - windows[g], start + tok_rows, start, windows[g]]).astype(jnp.int32)
        offsets = jnp.arange(n, dtype=jnp.int32) * tok_rows
        kt, va = lay_out_keys([pack], [offsets], span)
        mine = queries[:, g * per_group : (g + 1) * per_group]
        attended.append(attend(mine, kt, va, span, list(range(tok_rows // TQ))))
    attended = jnp.concatenate(attended, axis=1)
    partial = jnp.dot(
        attended,
        lax.all_gather(out_weight, "seq", axis=1, tiled=True),
        preferred_element_type=jnp.float32,
    )
    return lax.psum_scatter(
        partial.astype(jnp.bfloat16), "head", scatter_dimension=1, tiled=True
    )


def body(queries, keys, values, windows, out_weight):
    tok_rows = queries.shape[0]
    s, h = lax.axis_index("seq"), lax.axis_index("head")
    depth, piece_cols = out_weight.shape
    width = out_weight.shape[1] * lax.axis_size("seq") // lax.axis_size("head")
    start = s * tok_rows
    span = jnp.stack([start - windows[0], start + tok_rows, start, windows[0]]).astype(jnp.int32)

    kv = jnp.concatenate([keys, values], axis=1)
    kd, kz, kx = swap(kv, 8), swap(kv, 4), swap(kv, 2)
    half = piece_cols // 2
    parts = [out_weight[:, :half], out_weight[:, half:]]
    far = [swap(part, 8) for part in parts]
    kdz = swap(kd, 4)
    kzd_x = swap(jnp.concatenate([kz, kd]), 2)
    kdz_x = swap(kdz, 2)
    near = jnp.concatenate([kv, kx, kz, kd])
    rest = jnp.concatenate([kzd_x, kdz, kdz_x])
    near_c, rest_c = swap(near, 1), swap(rest, 1)
    near_bits = jnp.array([0, 2, 4, 8], jnp.int32)
    rest_bits = jnp.array([6, 10, 12, 14], jnp.int32)
    offsets = [(s ^ b) * tok_rows for b in (near_bits, rest_bits, near_bits ^ 1, rest_bits ^ 1)]

    home = (s >= lax.axis_size("seq") // 2) == (h == 1)
    own_rows = [jnp.where(home, p, f) for p, f in zip(parts, far)]
    other_rows = [swap_head(jnp.where(home, f, p)) for p, f in zip(parts, far)]

    units = []
    for g in (0, 1):
        sides = []
        for rows in (own_rows[g], other_rows[g]):
            by_x, by_z = swap(rows, 2), swap(rows, 4)
            corner = [swap(by_z[: depth // 2], 2), swap(by_x[depth // 2 :], 4)]
            sides.append([[rows], [by_x], [by_z], corner])
        units.append([(sides[0][k], sides[1][k]) for k in range(4)])

    kt, va = lay_out_keys([near, rest, near_c, rest_c], offsets, span)
    attended = None
    for t in range(tok_rows // TQ):
        attended = attend(queries, kt, va, span, [t], attended)
    other_head = swap_head(attended)
    both = [attended, other_head, swap(attended, 1), swap(other_head, 1)]

    def columns(bits, g, core):
        at = s ^ jnp.array(bits, jnp.int32)
        zx = (at // 2) % 4
        return ((zx * 2 + (at + core) % 2) * 2 + g).astype(jnp.int32)

    out, received, place = None, [], []
    for g, ks in ((0, (0, 1, 2, 3)), (1, (0, 1, 2)), (1, (3,))):
        bits = [(0, 2, 4, 6)[k] for k in ks]
        out, send = project(both, [units[g][k] for k in ks], columns(bits, g, 0), width, out)
        received.append(swap(send, 1))
        place.append(columns(bits, g, 1))
    return put_blocks(out, received, jnp.concatenate(place))


def solution(mesh):
    placed = (P("seq", "head"), P("seq", "head"), P("seq", "head"), P("head"), P("head", "seq"))
    known = mesh.shape["seq"] == 16 and mesh.shape["head"] == 2
    return jax.shard_map(
        body if known else body_any,
        mesh=mesh,
        in_specs=placed,
        out_specs=P("seq", "head"),
        check_vma=False,
    )
```
